256 devices in a mesh: row: 16 (over y, z_lo, core), col: 16 (over x, z_hi).
Axes of the slice: x: 4, y: 4, z: 8 (z_hi: 4, z_lo: 2; z = z_hi * 2 + z_lo), core: 2. Of those that a mesh axis runs over, the one named last changes fastest.
Arguments:
- points: float32 [32, 24576], P(None, ('row', 'col')), may hold values from -6 to 6
- targets: float32 [24576], P(('row', 'col')), may hold values from -6 to 6
- probes: float32 [8, 24576], P(None, ('row', 'col')), may hold values from -6 to 6
- lengthscale: float32 [4], replicated, may hold values from 2.4 to 3.4
- outputscale: float32 [4], replicated, may hold values from 0.5 to 2
- noise_var: float32 [4], replicated, may hold values from 0.1 to 1
Outputs:
- solution: float32 [12, 24576], P(None, ('row', 'col'))
- residual: float32 [12, 24576], P(None, ('row', 'col'))
The draws below stay inside these ranges and needn't reach their ends.
All inputs are finite; a program needn't handle non-finite values.
Results may differ from the reference program's by a relative error of at most 0.009.
Values may be sent and summed in bfloat16 or wider, within the bound.
A program may use at most 64 MiB of HBM per device.

```python
import math
import jax
import jax.numpy as jnp
from jax import lax

FEATURES = 32
PARTICLES = 4
PROBES = 2
ITERATIONS = 2
POINTS = 24576


def levels(key, dims, shards, least, top_value):
    level, own = 1.0, jax.random.fold_in(key, 6)
    for axis_at, parts in shards:
        steps = jnp.exp(jax.random.uniform(jax.random.fold_in(own, axis_at), (parts,), jnp.float32, least / len(shards), top_value / len(shards)))
        level = level * jnp.repeat(steps, dims[axis_at] // parts).reshape([-1 if axis == axis_at else 1 for axis in range(len(dims))])
    return level


def scatter_about(rng, extent, spread, reach, pieces=(), held_as=jnp.bfloat16):
    factor_of = levels(rng, extent, pieces, -0.22, 0.18) if pieces else 1.0
    result = jax.random.normal(rng, extent, jnp.float32) * spread * factor_of
    return jnp.minimum(jnp.maximum(result, -reach), reach).astype(held_as)


def setup_inputs(seed: int = 0) -> dict:
    splits = jax.random.split(jax.random.key(seed), 7)
    return {
        "points": scatter_about(splits[0], (FEATURES, POINTS), 1.0, 6.0, ((1, 256),), jnp.float32),
        "targets": scatter_about(splits[1], (POINTS,), 1.0, 6.0, ((0, 256),), jnp.float32),
        "probes": scatter_about(splits[2], (PARTICLES * PROBES, POINTS), 1.0, 6.0, ((1, 256),), jnp.float32),
        "lengthscale": jnp.clip(jnp.exp(jax.random.uniform(splits[3], (PARTICLES,), jnp.float32, math.log(2.4), math.log(3.4))), 2.4, 3.4),
        "outputscale": jnp.clip(jnp.exp(jax.random.uniform(splits[4], (PARTICLES,), jnp.float32, math.log(0.5), math.log(2.0))), 0.5, 2.0),
        "noise_var": jnp.clip(jnp.exp(jax.random.uniform(splits[5], (PARTICLES,), jnp.float32, math.log(0.1), math.log(1.0))), 0.1, 1.0),
    }


def sq_distance(rows_x, cols_x):
    inner_prod = lax.dot_general(rows_x, cols_x, (((0,), (0,)), ((), ())), precision=lax.Precision.HIGHEST, preferred_element_type=jnp.float32)
    sq_rows = jnp.sum(rows_x * rows_x, axis=0)
    sq_cols = jnp.sum(cols_x * cols_x, axis=0)
    return (sq_rows[:, None] + sq_cols[None, :]) - 2.0 * inner_prod


def kernel_rows(distance, dir_cols, negscale, outputscale, width):
    products = []
    for p in range(negscale.shape[0]):
        kern_tile = (outputscale[p] * jnp.exp(distance * negscale[p])).astype(jnp.bfloat16)
        products.append(lax.dot_general(dir_cols[p * width:(p + 1) * width], kern_tile, (((1,), (1,)), ((), ())), preferred_element_type=jnp.float32))
    return jnp.concatenate(products, axis=0)


def apply_full(points, dir_low, negscale, outputscale, width):
    total = points.shape[1]
    row_block = math.gcd(total, 1024)

    def one_block(start):
        rows_x = lax.dynamic_slice_in_dim(points, start, row_block, 1)
        distance = sq_distance(rows_x, points)
        return kernel_rows(distance, dir_low, negscale, outputscale, width)

    starts = jnp.arange(total // row_block, dtype=jnp.int32) * row_block
    blocks = lax.map(one_block, starts)
    return jnp.transpose(blocks, (1, 0, 2)).reshape(blocks.shape[1], total)


def reference(points, targets, probes, lengthscale, outputscale, noise_var):
    n_part = lengthscale.shape[0]
    width = probes.shape[0] // n_part + 1
    right_side = jnp.concatenate([jnp.concatenate([targets[None, :], probes[p * (width - 1):(p + 1) * (width - 1)]], axis=0) for p in range(n_part)], axis=0)
    negscale = -0.5 / (lengthscale * lengthscale)
    noisevec = jnp.repeat(noise_var, width)[:, None]
    solution = jnp.zeros_like(right_side)
    residual = right_side
    direction = right_side
    res_norm = jnp.sum(residual * residual, axis=1)
    for iteration in range(ITERATIONS):
        dir_low = direction.astype(jnp.bfloat16)
        applied = apply_full(points, dir_low, negscale, outputscale, width) + noisevec * direction
        curvature = jnp.sum(direction * applied, axis=1)
        step_size = (res_norm / curvature)[:, None]
        solution = solution + step_size * direction
        residual = residual - step_size * applied
        if iteration + 1 < ITERATIONS:
            fresh_norm = jnp.sum(residual * residual, axis=1)
            direction = residual + (fresh_norm / res_norm)[:, None] * direction
            res_norm = fresh_norm
    return (solution, residual)
```

```python
import functools
import math

import jax
import jax.numpy as jnp
from jax import lax
from jax.experimental import pallas as pl
from jax.experimental.pallas import tpu as pltpu
from jax.sharding import PartitionSpec as P

ITERATIONS = 2
ROWS = 16
LANES = 128
TILE = 256
LOG2E = math.log2(math.e)
F32 = jnp.float32
BF16 = jnp.bfloat16
MESH = pl.DeviceIdType.MESH


def split3(x):
    hi = x.astype(BF16).astype(F32)
    rest = x - hi
    mid = rest.astype(BF16).astype(F32)
    low = (rest - mid).astype(BF16).astype(F32)
    return hi, mid, low


def norm_rows(parts, ones_first):
    at = lax.broadcasted_iota(jnp.int32, (16, parts[0].shape[1]), 0)
    start = 3 if ones_first else 0
    out = jnp.where((at < 3) if ones_first else ((at >= 3) & (at < 6)), 1.0, 0.0).astype(F32)
    for k in range(3):
        out = jnp.where(at == start + k, parts[k], out)
    return out


def compact(dst, slots, first, rows, count, width):
    for k in range(count):
        dst[:, k * width : (k + 1) * width] = slots[k, first : first + rows, :width]


def kernel(
    n_red,
    n_con,
    width,
    per,
    points,
    targets,
    probes,
    lengthscale,
    outputscale,
    noise_var,
    sol_out,
    res_out,
    msg,
    con_in,
    red_in,
    con_lhs,
    red_x,
    red_rhs,
    con_d,
    red_d,
    con_a,
    red_a,
    blocks,
    kept,
    product,
    rs_send,
    rs_recv,
    ag_send,
    ag_con,
    ag_red,
    nrm_send,
    nrm_recv,
    rs2_send,
    rs2_recv,
    fin_send,
    fin_recv,
    send_sem,
    recv_sem,
):
    n_part = lengthscale.shape[0]
    feats = points.shape[0]
    count = n_part * per
    span = n_con * width
    wide = n_red * width
    me_red = lax.axis_index("row")
    me_con = lax.axis_index("col")

    def red_peer(step):
        at = lax.rem(me_red + step, n_red)
        return at, (at, me_con)

    def con_peer(step):
        at = lax.rem(me_con + step, n_con)
        return at, (me_red, at)

    barrier = pltpu.get_barrier_semaphore()
    for step in range(1, n_red):
        pl.semaphore_signal(barrier, inc=1, device_id=red_peer(step)[1], device_id_type=MESH)
    for step in range(1, n_con):
        pl.semaphore_signal(barrier, inc=1, device_id=con_peer(step)[1], device_id_type=MESH)

    msg[...] = jnp.zeros_like(msg)
    msg[0:feats, 0:width] = points[...]
    for p in range(n_part):
        at = feats + p * per
        msg[at : at + 1, 0:width] = targets[...]
        msg[at + 1 : at + per, 0:width] = probes[p * (per - 1) : (p + 1) * (per - 1), :]

    row_at = lax.broadcasted_iota(jnp.int32, (ROWS, 1), 0)
    lane_at = lax.broadcasted_iota(jnp.int32, (ROWS, LANES), 1)
    live = row_at < count
    noise = jnp.zeros((ROWS, 1), F32)
    for p in range(n_part):
        noise = jnp.where((row_at >= p * per) & (row_at < (p + 1) * per), noise_var[p], noise)

    pl.semaphore_wait(barrier, n_red - 1 + n_con - 1)

    def send(phase, peer, src, dst):
        pltpu.make_async_remote_copy(
            src_ref=src,
            dst_ref=dst,
            send_sem=send_sem.at[phase],
            recv_sem=recv_sem.at[phase],
            device_id=peer,
            device_id_type=MESH,
        ).start()

    def to_con(phase, src, slots):
        for step in range(1, n_con):
            send(phase, con_peer(step)[1], src, slots.at[me_con])

    def to_red(phase, src, slots):
        for step in range(1, n_red):
            send(phase, red_peer(step)[1], src, slots.at[me_red])

    def arrive(sem, slots, n):
        some = slots.at[pl.ds(0, n - 1)]
        pltpu.make_async_copy(some, some, sem).wait()

    to_con(0, msg, con_in)
    to_red(1, msg, red_in)
    con_in[me_con] = msg[...]
    red_in[me_red] = msg[...]
    arrive(recv_sem.at[0], con_in, n_con)

    pad = jnp.zeros((TILE - 6 * feats - 16, LANES), F32)

    def con_block(k, _):
        x = con_in[k, 0:feats, :]
        hi, mid, low = split3(x)
        norms = norm_rows(split3(jnp.sum(x * x, axis=0, keepdims=True)), False)
        full = jnp.concatenate([hi, hi, mid, hi, mid, low, norms, pad], axis=0)
        con_lhs[pl.ds(pl.multiple_of(k * width, 32), width), :] = jnp.transpose(full)[0:width].astype(BF16)
        return 0

    lax.fori_loop(0, n_con, con_block, 0)
    compact(con_d, con_in, feats, ROWS, n_con, width)

    def spread(direction):
        for p in range(n_part):
            mine = (row_at >= p * per) & (row_at < (p + 1) * per)
            blocks[:, p * span : (p + 1) * span] = jnp.where(mine, direction, 0.0).astype(BF16)

    spread(con_d[...])

    arrive(recv_sem.at[1], red_in, n_red)
    compact(red_x, red_in, 0, feats, n_red, width)
    compact(red_d, red_in, feats, ROWS, n_red, width)
    x = red_x[...]
    hi, mid, low = split3(x)
    norms = norm_rows(split3(jnp.sum(x * x, axis=0, keepdims=True)), True)
    hi, mid, low = (-2.0 * hi, -2.0 * mid, -2.0 * low)
    pad2 = jnp.zeros((TILE - 6 * feats - 16, wide), F32)
    red_rhs[...] = jnp.concatenate([hi, mid, hi, low, mid, hi, norms, pad2], axis=0).astype(BF16)

    scales = []
    for p in range(n_part):
        length = jnp.full((1, TILE), lengthscale[p], F32)
        scales.append(((-0.5 * LOG2E) / (length * length), jnp.full((1, TILE), outputscale[p], F32)))

    product[...] = jnp.zeros_like(product)

    def build(ib, _):
        at = pl.multiple_of(ib * TILE, TILE)
        lhs = con_lhs[pl.ds(at, TILE), :]
        for jb in range(wide // TILE):
            cols = slice(jb * TILE, (jb + 1) * TILE)
            distance = jnp.dot(lhs, red_rhs[:, cols], preferred_element_type=F32)
            total = product[:, cols]
            for p in range(n_part):
                kern = (scales[p][1] * jnp.exp2(distance * scales[p][0])).astype(BF16)
                here = pl.ds(pl.multiple_of(p * span + at, TILE), TILE)
                kept[here, cols] = kern
                total = total + jnp.dot(blocks[:, here], kern, preferred_element_type=F32)
            product[:, cols] = total
        return 0

    lax.fori_loop(0, span // TILE, build, 0)

    def scatter(phase, buf, slots, extra):
        for k in range(n_red):
            part = product[:, k * width : (k + 1) * width]
            buf[k, :, 0:width] = part
            buf[k, :, width:LANES] = jnp.broadcast_to(extra, (ROWS, LANES - width))
        for step in range(1, n_red):
            at, peer = red_peer(step)
            send(phase, peer, buf.at[at], slots.at[me_red])
        slots[me_red] = buf[me_red]
        arrive(recv_sem.at[phase], slots, n_red)
        return jnp.sum(slots[...], axis=0)

    mid_lane = (width + LANES) // 2
    own_d = msg[feats : feats + ROWS, :]
    d_con = con_d[...]
    d_red = red_d[...]
    a_own = scatter(2, rs_send, rs_recv, jnp.sum(d_red * product[...], axis=1, keepdims=True))
    a_own = a_own + jnp.where(lane_at < width, noise * own_d, 0.0)
    norm_red = jnp.sum(d_red * d_red, axis=1, keepdims=True)
    ag_send[...] = jnp.where(lane_at < mid_lane, a_own, norm_red)
    to_con(3, ag_send, ag_con)
    to_red(4, ag_send, ag_red)
    ag_con[me_con] = ag_send[...]
    ag_red[me_red] = ag_send[...]

    def totals(slots):
        total = jnp.sum(slots[...], axis=0)
        return total[:, width : width + 1], total[:, mid_lane : mid_lane + 1]

    arrive(recv_sem.at[3], ag_con, n_con)
    curve_kern, res_norm = totals(ag_con)
    curvature = curve_kern + noise * res_norm
    step_size = res_norm / jnp.where(live, curvature, 1.0)
    compact(con_a, ag_con, 0, ROWS, n_con, width)
    r_con = d_con - step_size * con_a[...]
    nrm_send[...] = jnp.broadcast_to(jnp.sum(r_con * r_con, axis=1, keepdims=True), (ROWS, LANES))
    to_red(5, nrm_send, nrm_recv)
    nrm_recv[me_red] = nrm_send[...]
    arrive(recv_sem.at[4], ag_red, n_red)
    compact(red_a, ag_red, 0, ROWS, n_red, width)
    r_red = d_red - step_size * red_a[...]
    arrive(recv_sem.at[5], nrm_recv, n_red)
    fresh_norm = jnp.sum(nrm_recv[...], axis=0)[:, 0:1]
    beta = fresh_norm / jnp.where(live, res_norm, 1.0)
    spread(r_con + beta * d_con)
    d1_red = r_red + beta * d_red
    r_own = own_d - step_size * a_own
    d1_own = r_own + beta * own_d

    for jb in range(wide // TILE):
        cols = slice(jb * TILE, (jb + 1) * TILE)
        product[:, cols] = jnp.dot(blocks[...], kept[:, cols], preferred_element_type=F32)

    a1_own = scatter(6, rs2_send, rs2_recv, jnp.sum(d1_red * product[...], axis=1, keepdims=True))
    norm1_red = jnp.sum(d1_red * d1_red, axis=1, keepdims=True)
    fin_send[...] = jnp.where(lane_at < mid_lane, a1_own, norm1_red)
    to_con(7, fin_send, fin_recv)
    fin_recv[me_con] = fin_send[...]
    a1_own = a1_own + noise * d1_own
    arrive(recv_sem.at[7], fin_recv, n_con)
    curve_kern1, d1_norm = totals(fin_recv)
    curvature1 = curve_kern1 + noise * d1_norm
    step1 = fresh_norm / jnp.where(live, curvature1, 1.0)
    sol = step_size * own_d + step1 * d1_own
    res = r_own - step1 * a1_own
    sol_out[...] = sol[0:count, 0:width]
    res_out[...] = res[0:count, 0:width]

    for phase, slots, n in (
        (0, con_in, n_con),
        (1, red_in, n_red),
        (2, rs_recv, n_red),
        (3, ag_con, n_con),
        (4, ag_red, n_red),
        (5, nrm_recv, n_red),
        (6, rs2_recv, n_red),
        (7, fin_recv, n_con),
    ):
        arrive(send_sem.at[phase], slots, n)


def solution(mesh):
    n_red, n_con = mesh.shape["row"], mesh.shape["col"]

    def on_device(points, targets, probes, lengthscale, outputscale, noise_var):
        feats, width = points.shape
        n_part = lengthscale.shape[0]
        per = probes.shape[0] // n_part + 1
        count = n_part * per
        span, wide = n_con * width, n_red * width
        vmem = pl.BlockSpec(memory_space=pltpu.VMEM)
        smem = pl.BlockSpec(memory_space=pltpu.SMEM)
        out = jax.ShapeDtypeStruct((count, width), F32)

        def slots(n):
            return pltpu.VMEM((n, ROWS, LANES), F32)

        return pl.pallas_call(
            functools.partial(kernel, n_red, n_con, width, per),
            out_shape=(out, out),
            in_specs=[vmem] * 3 + [smem] * 3,
            out_specs=(vmem, vmem),
            scratch_shapes=[
                pltpu.VMEM((feats + ROWS, LANES), F32),
                pltpu.VMEM((n_con, feats + ROWS, LANES), F32),
                pltpu.VMEM((n_red, feats + ROWS, LANES), F32),
                pltpu.VMEM((span, TILE), BF16),
                pltpu.VMEM((feats, wide), F32),
                pltpu.VMEM((TILE, wide), BF16),
                pltpu.VMEM((ROWS, span), F32),
                pltpu.VMEM((ROWS, wide), F32),
                pltpu.VMEM((ROWS, span), F32),
                pltpu.VMEM((ROWS, wide), F32),
                pltpu.VMEM((ROWS, n_part * span), BF16),
                pltpu.VMEM((n_part * span, wide), BF16),
                pltpu.VMEM((ROWS, wide), F32),
                slots(n_red),
                slots(n_red),
                pltpu.VMEM((ROWS, LANES), F32),
                slots(n_con),
                slots(n_red),
                pltpu.VMEM((ROWS, LANES), F32),
                slots(n_red),
                slots(n_red),
                slots(n_red),
                pltpu.VMEM((ROWS, LANES), F32),
                slots(n_con),
                pltpu.SemaphoreType.DMA((8,)),
                pltpu.SemaphoreType.DMA((8,)),
            ],
            compiler_params=pltpu.CompilerParams(
                collective_id=0, has_side_effects=True, vmem_limit_bytes=56 * 2**20
            ),
            name="cg_solve",
        )(points, targets[None, :], probes, lengthscale, outputscale, noise_var)

    both = P(None, ("row", "col"))
    return jax.shard_map(
        on_device,
        mesh=mesh,
        in_specs=(both, P(("row", "col")), both, P(), P(), P()),
        out_specs=(both, both),
        check_vma=False,
    )
```

```python
import functools
import math

import jax
import jax.numpy as jnp
from jax import lax
from jax.experimental import pallas as pl
from jax.experimental.pallas import tpu as pltpu
from jax.sharding import PartitionSpec as P

LANES = 128
TILE = 256
CHUNK = 32
LOG2E = math.log2(math.e)
F32 = jnp.float32
BF16 = jnp.bfloat16
MESH = pl.DeviceIdType.MESH
NX, NY, NZ, CORES = 4, 4, 8, 2


def split3(x):
    hi = x.astype(BF16).astype(F32)
    rest = x - hi
    mid = rest.astype(BF16).astype(F32)
    low = (rest - mid).astype(BF16).astype(F32)
    return hi, mid, low


def norm_rows(parts, ones_first):
    at = lax.broadcasted_iota(jnp.int32, (16, parts[0].shape[1]), 0)
    start = 3 if ones_first else 0
    out = jnp.where((at < 3) if ones_first else ((at >= 3) & (at < 6)), 1.0, 0.0).astype(F32)
    for k in range(3):
        out = jnp.where(at == start + k, parts[k], out)
    return out


def kernel(
    width,
    per,
    points_hbm,
    targets_hbm,
    probes_hbm,
    lengthscale_hbm,
    outputscale_hbm,
    noise_hbm,
    sol_out,
    res_out,
    points,
    targets,
    probes,
    lengthscale,
    outputscale,
    noise_var,
    rhs,
    msg,
    con_in,
    red_in,
    red_rhs_in,
    con_lhs,
    con_dt,
    red_x,
    red_op,
    con_d,
    red_d,
    con_a,
    red_a,
    blocks,
    dist,
    kept,
    product,
    rs_send,
    rs_recv,
    ag_send,
    ag_con,
    ag_red,
    nrm_send,
    nrm_recv,
    rs2_send,
    rs2_recv,
    crv_send,
    crv_recv,
    fin_send,
    fin_recv,
    load_sem,
    send_sem,
    recv_sem,
    con_sem,
):
    n_red, n_con = NX * NY, NZ * CORES
    n_part = lengthscale.shape[0]
    feats = points.shape[0]
    groups = feats // 8
    count = n_part * per
    pair = CORES * width
    span = n_con * width
    wide = n_red * width
    base = feats * width // 8

    loads = [
        pltpu.make_async_copy(a, b, load_sem.at[k])
        for k, (a, b) in enumerate(
            (
                (points_hbm, points),
                (targets_hbm, targets),
                (probes_hbm, probes),
                (lengthscale_hbm, lengthscale),
                (outputscale_hbm, outputscale),
                (noise_hbm, noise_var),
            )
        )
    ]
    for load in loads:
        load.start()

    at_row, at_col = lax.axis_index("row"), lax.axis_index("col")
    at_y, z_lo, core = at_row // 4, lax.rem(at_row // 2, 2), lax.rem(at_row, 2)
    at_x, z_hi = at_col // 4, lax.rem(at_col, 4)
    at_z = z_hi * 2 + z_lo
    me_red, me_con = at_x * NY + at_y, at_z * CORES + core

    def red_peer(step):
        at = lax.rem(me_red + step, n_red)
        return at, (lax.rem(at, NY) * 4 + z_lo * 2 + core, (at // NY) * 4 + z_hi)

    def near_z(t):
        away = ((t + 1) // 2) * (2 * lax.rem(t, 2) - 1)
        return lax.rem(at_z + away + NZ, NZ)

    def con_peer(z, c):
        return z * CORES + c, (at_y * 4 + lax.rem(z, 2) * 2 + c, at_x * 4 + z // 2)

    near = [near_z(t) for t in range(NZ)]
    con_peers = [con_peer(at_z, 1 - core)]
    for t in range(1, NZ):
        con_peers += [con_peer(near[t], core), con_peer(near[t], 1 - core)]
    red_peers = [red_peer(step) for step in range(1, n_red)]

    def arrive(sem, slots, n):
        some = slots.at[pl.ds(0, n - 1)]
        pltpu.make_async_copy(some, some, sem).wait()

    def drain(phases):
        buffers = (con_in, red_in, rs_recv, ag_con, ag_red, nrm_recv, rs2_recv, fin_recv, crv_recv, red_rhs_in)
        for phase in phases:
            arrive(send_sem.at[phase], buffers[phase], buffers[phase].shape[0])

    barrier = pltpu.get_barrier_semaphore()
    for _, peer in con_peers + red_peers:
        pl.semaphore_signal(barrier, inc=1, device_id=peer, device_id_type=MESH)

    msg[...] = jnp.zeros_like(msg)
    rhs[...] = jnp.zeros_like(rhs)
    for load in loads:
        load.wait()
    for q in range(groups):
        msg[:, q * width : (q + 1) * width] = points[8 * q : 8 * q + 8, :]
    for p in range(n_part):
        rhs[p * per : p * per + 1, 0:width] = targets[...]
        rhs[p * per + 1 : (p + 1) * per, 0:width] = probes[p * (per - 1) : (p + 1) * (per - 1), :]
    msg[:, base : base + width] = rhs[0:8, 0:width]
    msg[0 : count - 8, base + width : base + 2 * width] = rhs[8:count, 0:width]

    row_at = lax.broadcasted_iota(jnp.int32, (count, 1), 0)
    lane_at = lax.broadcasted_iota(jnp.int32, (count, LANES), 1)
    mine = [(row_at >= p * per) & (row_at < (p + 1) * per) for p in range(n_part)]
    noise = jnp.zeros((count, 1), F32)
    for p in range(n_part):
        noise = jnp.where(mine[p], noise_var[p], noise)
    scales = []
    for p in range(n_part):
        length = jnp.full((1, TILE), lengthscale[p], F32)
        scales.append(((-0.5 * LOG2E) / (length * length), jnp.full((1, TILE), outputscale[p], F32)))
    product[...] = jnp.zeros_like(product)

    pl.semaphore_wait(barrier, n_red - 1 + n_con - 1)

    def send(phase, peer, src, dst, sem=None):
        pltpu.make_async_remote_copy(
            src_ref=src,
            dst_ref=dst,
            send_sem=send_sem.at[phase],
            recv_sem=recv_sem.at[phase] if sem is None else sem,
            device_id=peer,
            device_id_type=MESH,
        ).start()

    def to_con(phase, src, slots):
        for _, peer in con_peers:
            send(phase, peer, src, slots.at[me_con])

    def to_red(phase, src, slots):
        for _, peer in red_peers:
            send(phase, peer, src, slots.at[me_red])

    for _, peer in con_peers[:5]:
        send(0, peer, msg, con_in.at[me_con], con_sem.at[me_con])
    to_red(1, msg.at[:, 0:base], red_in)
    for _, peer in con_peers[5:]:
        send(0, peer, msg, con_in.at[me_con], con_sem.at[me_con])
    to_red(9, msg.at[:, base:], red_rhs_in)
    con_in[me_con] = msg[...]
    red_in[me_red] = msg[:, 0:base]
    red_rhs_in[me_red] = msg[:, base:]

    pad = jnp.zeros((TILE - 6 * feats - 16, LANES), F32)

    def con_wait(slot):
        pltpu.make_async_copy(con_in.at[slot], con_in.at[slot], con_sem.at[slot]).wait()

    def prepare(t, z, buf):
        for c in range(CORES):
            slot = z * CORES + c
            x = jnp.concatenate(
                [con_in[slot, :, q * width : q * width + LANES] for q in range(groups)], axis=0
            )
            hi, mid, low = split3(x)
            norms = norm_rows(split3(jnp.sum(x * x, axis=0, keepdims=True)), False)
            full = jnp.concatenate([hi, hi, mid, hi, mid, low, norms, pad], axis=0)
            con_lhs[buf, c * width : (c + 1) * width, :] = jnp.transpose(full)[0:width].astype(BF16)
            con_dt[t, 0:8, c * width : (c + 1) * width] = con_in[slot, :, base : base + width]
            con_dt[t, 8:count, c * width : (c + 1) * width] = con_in[
                slot, 0 : count - 8, base + width : base + 2 * width
            ]

    def build(t, buf):
        low = con_dt[t, :, 0:pair]
        sides = [jnp.where(mine[p], low, 0.0).astype(BF16) for p in range(n_part)]
        lhs = con_lhs[buf]
        for jb in range(wide // TILE):
            cols = slice(jb * TILE, (jb + 1) * TILE)
            dist[jb] = jnp.dot(lhs, red_op[:, cols], preferred_element_type=F32)
        for jb in range(wide // TILE):
            cols = slice(jb * TILE, (jb + 1) * TILE)
            for r in range(pair // CHUNK):
                part = dist[jb, r * CHUNK : (r + 1) * CHUNK, :]
                for p in range(n_part):
                    kern = (scales[p][1] * jnp.exp2(part * scales[p][0])).astype(BF16)
                    at = pl.multiple_of(p * span + t * pair + r * CHUNK, CHUNK)
                    kept[pl.ds(at, CHUNK), cols] = kern
            total = product[:, cols]
            for p in range(n_part):
                at = pl.multiple_of(p * span + t * pair, CHUNK)
                total = total + jnp.dot(sides[p], kept[pl.ds(at, pair), cols], preferred_element_type=F32)
            product[:, cols] = total

    con_wait(at_z * CORES + 1 - core)
    prepare(0, at_z, 0)

    arrive(recv_sem.at[1], red_in, n_red)
    for k in range(n_red):
        for q in range(groups):
            red_x[8 * q : 8 * q + 8, k * width : (k + 1) * width] = red_in[k, :, q * width : (q + 1) * width]
    x = red_x[...]
    hi, mid, low = split3(x)
    norms = norm_rows(split3(jnp.sum(x * x, axis=0, keepdims=True)), True)
    hi, mid, low = (-2.0 * hi, -2.0 * mid, -2.0 * low)
    pad2 = jnp.zeros((TILE - 6 * feats - 16, wide), F32)
    red_op[...] = jnp.concatenate([hi, mid, hi, low, mid, hi, norms, pad2], axis=0).astype(BF16)

    def step(t, _):
        z = near_z(t + 1)
        con_wait(z * CORES)
        con_wait(z * CORES + 1)
        build(t, lax.rem(t, 2))
        prepare(t + 1, z, lax.rem(t + 1, 2))
        return 0

    lax.fori_loop(0, NZ - 1, step, 0)
    build(NZ - 1, (NZ - 1) % 2)

    arrive(recv_sem.at[9], red_rhs_in, n_red)
    for k in range(n_red):
        red_d[0:8, k * width : (k + 1) * width] = red_rhs_in[k, :, 0:width]
        red_d[8:count, k * width : (k + 1) * width] = red_rhs_in[k, 0 : count - 8, width : 2 * width]

    def chunk_out(k, buf, extra):
        buf[k, :, 0:width] = product[:, k * width : (k + 1) * width]
        buf[k, :, width:LANES] = jnp.broadcast_to(extra, (count, LANES - width))

    def to_row(column, offset):
        return jnp.sum(jnp.where(lane_at == row_at + offset, column, 0.0), axis=0, keepdims=True)

    def to_column(row, offset):
        return jnp.sum(jnp.where(lane_at == row_at + offset, row, 0.0), axis=1, keepdims=True)

    mid_lane = (width + LANES) // 2
    own_d = rhs[...]
    d_red = red_d[...]
    partial_curve = jnp.sum(d_red * product[...], axis=1, keepdims=True)
    for k in range(n_red):
        chunk_out(k, rs_send, partial_curve)
    for at, peer in red_peers:
        send(2, peer, rs_send.at[at], rs_recv.at[me_red])
    rs_recv[me_red] = rs_send[me_red]
    for t in range(NZ):
        con_d[:, t * pair : (t + 1) * pair] = con_dt[t, :, 0:pair]
    d_con = con_d[...]
    norm_red = jnp.sum(d_red * d_red, axis=1, keepdims=True)
    arrive(recv_sem.at[2], rs_recv, n_red)
    a_own = jnp.sum(rs_recv[...], axis=0)
    a_own = a_own + jnp.where(lane_at < width, noise * own_d, 0.0)
    ag_send[...] = jnp.where(lane_at < mid_lane, a_own, norm_red)
    to_con(3, ag_send, ag_con)
    to_red(4, ag_send, ag_red)
    ag_con[me_con] = ag_send[...]
    ag_red[me_red] = ag_send[...]

    arrive(recv_sem.at[3], ag_con, n_con)
    total = jnp.sum(ag_con[...], axis=0)
    res_norm = total[:, mid_lane : mid_lane + 1]
    curvature = total[:, width : width + 1] + noise * res_norm
    step_size = res_norm / curvature
    for t in range(NZ):
        for c in range(CORES):
            at = t * pair + c * width
            con_a[:, at : at + width] = ag_con[near[t] * CORES + c, :, 0:width]
    r_con = d_con - step_size * con_a[...]
    nrm_send[...] = to_row(jnp.sum(r_con * r_con, axis=1, keepdims=True), 0)
    to_red(5, nrm_send, nrm_recv)
    nrm_recv[me_red] = nrm_send[...]
    arrive(recv_sem.at[4], ag_red, n_red)
    for k in range(n_red):
        red_a[:, k * width : (k + 1) * width] = ag_red[k, :, 0:width]
    r_red = d_red - step_size * red_a[...]
    r_own = own_d - step_size * a_own
    arrive(recv_sem.at[5], nrm_recv, n_red)
    fresh_norm = to_column(jnp.sum(nrm_recv[...], axis=0), 0)
    beta = fresh_norm / res_norm
    d1_con = r_con + beta * d_con
    for p in range(n_part):
        blocks[:, p * span : (p + 1) * span] = jnp.where(mine[p], d1_con, 0.0).astype(BF16)
    d1_red = r_red + beta * d_red
    d1_own = r_own + beta * own_d

    done = 0
    for jb in range(wide // TILE):
        cols = slice(jb * TILE, (jb + 1) * TILE)
        product[:, cols] = jnp.dot(blocks[...], kept[:, cols], preferred_element_type=F32)
        while (done + 1) * width <= (jb + 1) * TILE:
            chunk_out(done, rs2_send, jnp.zeros((count, 1), F32))
            done += 1
    crv_send[...] = to_row(jnp.sum(d1_red * product[...], axis=1, keepdims=True), 0)
    to_red(8, crv_send, crv_recv)
    for at, peer in red_peers:
        send(6, peer, rs2_send.at[at], rs2_recv.at[me_red])
    crv_recv[me_red] = crv_send[...]
    norm1 = to_row(jnp.sum(d1_red * d1_red, axis=1, keepdims=True), count)
    arrive(recv_sem.at[8], crv_recv, n_red)
    fin_send[...] = jnp.sum(crv_recv[...], axis=0) + norm1
    to_con(7, fin_send, fin_recv)
    fin_recv[me_con] = fin_send[...]
    rs2_recv[me_red] = rs2_send[me_red]
    arrive(recv_sem.at[6], rs2_recv, n_red)
    a1_own = jnp.sum(rs2_recv[...], axis=0) + noise * d1_own
    drain((0, 1, 2, 3, 4, 5, 6, 8, 9))
    arrive(recv_sem.at[7], fin_recv, n_con)
    total = jnp.sum(fin_recv[...], axis=0)
    step1 = fresh_norm / (to_column(total, 0) + noise * to_column(total, count))
    sol = step_size * own_d + step1 * d1_own
    res = r_own - step1 * a1_own
    sol_out[...] = sol[:, 0:width]
    res_out[...] = res[:, 0:width]
    drain((7,))


def solution(mesh):
    n_red, n_con = NX * NY, NZ * CORES

    def on_device(points, targets, probes, lengthscale, outputscale, noise_var):
        feats, width = points.shape
        n_part = lengthscale.shape[0]
        per = probes.shape[0] // n_part + 1
        count = n_part * per
        pair, span, wide = CORES * width, n_con * width, n_red * width
        whole = pl.cdiv(feats * width // 8 + 2 * width, LANES) * LANES
        base = feats * width // 8
        vmem = pl.BlockSpec(memory_space=pltpu.VMEM)
        anywhere = pl.BlockSpec(memory_space=pl.ANY)
        out = jax.ShapeDtypeStruct((count, width), F32)

        def slots(n, *shape):
            return pltpu.VMEM((n, *(shape or (count, LANES))), F32)

        row = pltpu.VMEM((1, LANES), F32)
        return pl.pallas_call(
            functools.partial(kernel, width, per),
            out_shape=(out, out),
            in_specs=[anywhere] * 6,
            out_specs=(vmem, vmem),
            scratch_shapes=[
                pltpu.VMEM((feats, width), F32),
                pltpu.VMEM((1, width), F32),
                pltpu.VMEM(probes.shape, F32),
                pltpu.SMEM((n_part,), F32),
                pltpu.SMEM((n_part,), F32),
                pltpu.SMEM((n_part,), F32),
                pltpu.VMEM((count, LANES), F32),
                pltpu.VMEM((8, whole), F32),
                slots(n_con, 8, whole),
                slots(n_red, 8, base),
                slots(n_red, 8, whole - base),
                pltpu.VMEM((2, pair, TILE), BF16),
                pltpu.VMEM((NZ, count, TILE), F32),
                pltpu.VMEM((feats, wide), F32),
                pltpu.VMEM((TILE, wide), BF16),
                pltpu.VMEM((count, span), F32),
                pltpu.VMEM((count, wide), F32),
                pltpu.VMEM((count, span), F32),
                pltpu.VMEM((count, wide), F32),
                pltpu.VMEM((count, n_part * span), BF16),
                pltpu.VMEM((wide // TILE, pair, TILE), F32),
                pltpu.VMEM((n_part * span, wide), BF16),
                pltpu.VMEM((count, wide), F32),
                slots(n_red),
                slots(n_red),
                pltpu.VMEM((count, LANES), F32),
                slots(n_con),
                slots(n_red),
                row,
                slots(n_red, 1, LANES),
                slots(n_red),
                slots(n_red),
                row,
                slots(n_red, 1, LANES),
                row,
                slots(n_con, 1, LANES),
                pltpu.SemaphoreType.DMA((6,)),
                pltpu.SemaphoreType.DMA((10,)),
                pltpu.SemaphoreType.DMA((10,)),
                pltpu.SemaphoreType.DMA((n_con,)),
            ],
            compiler_params=pltpu.CompilerParams(
                collective_id=0, has_side_effects=True, vmem_limit_bytes=56 * 2**20
            ),
            name="cg_solve",
        )(points, targets[None, :], probes, lengthscale, outputscale, noise_var)

    both = P(None, ("row", "col"))
    return jax.shard_map(
        on_device,
        mesh=mesh,
        in_specs=(both, P(("row", "col")), both, P(), P(), P()),
        out_specs=(both, both),
        check_vma=False,
    )
```

```python
import functools
import math

import jax
import jax.numpy as jnp
from jax import lax
from jax.experimental import pallas as pl
from jax.experimental.pallas import tpu as pltpu
from jax.sharding import PartitionSpec as P

LANES = 128
TILE = 256
CHUNK = 32
LOG2E = math.log2(math.e)
F32 = jnp.float32
BF16 = jnp.bfloat16
MESH = pl.DeviceIdType.MESH
NX, NY, NZ, CORES = 4, 4, 8, 2


def split3(x):
    hi = x.astype(BF16).astype(F32)
    rest = x - hi
    mid = rest.astype(BF16).astype(F32)
    low = (rest - mid).astype(BF16).astype(F32)
    return hi, mid, low


def norm_rows(parts, ones_first):
    at = lax.broadcasted_iota(jnp.int32, (16, parts[0].shape[1]), 0)
    start = 3 if ones_first else 0
    out = jnp.where((at < 3) if ones_first else ((at >= 3) & (at < 6)), 1.0, 0.0).astype(F32)
    for k in range(3):
        out = jnp.where(at == start + k, parts[k], out)
    return out


def kernel(
    width,
    per,
    points_hbm,
    targets_hbm,
    probes_hbm,
    lengthscale_hbm,
    outputscale_hbm,
    noise_hbm,
    sol_out,
    res_out,
    points,
    targets,
    probes,
    lengthscale,
    outputscale,
    noise_var,
    rhs,
    msg,
    con_in,
    red_in,
    red_rhs_in,
    lhs_even,
    lhs_odd,
    con_dt,
    red_x,
    red_op,
    con_d,
    red_d,
    con_a,
    red_a,
    blocks,
    dist_even,
    dist_odd,
    kept_even,
    kept_odd,
    product,
    rs_send,
    rs_recv,
    ag_send,
    ag_con,
    ag_red,
    mom_send,
    mom_recv,
    sum_send,
    sum_recv,
    rs2_send,
    rs2_recv,
    crv_send,
    crv_recv,
    fin_send,
    fin_recv,
    load_sem,
    send_sem,
    recv_sem,
    con_sem,
):
    n_red, n_con = NX * NY, NZ * CORES
    n_part = lengthscale.shape[0]
    feats = points.shape[0]
    groups = feats // 8
    count = n_part * per
    pair = CORES * width
    span = n_con * width
    wide = n_red * width
    base = feats * width // 8

    loads = [
        pltpu.make_async_copy(a, b, load_sem.at[k])
        for k, (a, b) in enumerate(
            (
                (points_hbm, points),
                (targets_hbm, targets),
                (probes_hbm, probes),
                (lengthscale_hbm, lengthscale),
                (outputscale_hbm, outputscale),
                (noise_hbm, noise_var),
            )
        )
    ]
    for load in loads:
        load.start()

    at_row, at_col = lax.axis_index("row"), lax.axis_index("col")
    at_y, z_lo, core = at_row // 4, lax.rem(at_row // 2, 2), lax.rem(at_row, 2)
    at_x, z_hi = at_col // 4, lax.rem(at_col, 4)
    at_z = z_hi * 2 + z_lo
    me_red, me_con = at_x * NY + at_y, at_z * CORES + core

    def red_peer(step):
        at = lax.rem(me_red + step, n_red)
        return at, (lax.rem(at, NY) * 4 + z_lo * 2 + core, (at // NY) * 4 + z_hi)

    def near_z(t):
        away = ((t + 1) // 2) * (2 * lax.rem(t, 2) - 1)
        return lax.rem(at_z + away + NZ, NZ)

    def con_peer(z, c):
        return z * CORES + c, (at_y * 4 + lax.rem(z, 2) * 2 + c, at_x * 4 + z // 2)

    near = [near_z(t) for t in range(NZ)]
    con_peers = [con_peer(at_z, 1 - core)]
    for t in range(1, NZ):
        con_peers += [con_peer(near[t], core), con_peer(near[t], 1 - core)]
    red_peers = [red_peer(step) for step in range(1, n_red)]

    def arrive(sem, slots, n):
        some = slots.at[pl.ds(0, n - 1)]
        pltpu.make_async_copy(some, some, sem).wait()

    def drain(phases):
        buffers = (con_in, red_in, rs_recv, ag_con, ag_red, mom_recv, rs2_recv, fin_recv, crv_recv, red_rhs_in, sum_recv)
        for phase in phases:
            arrive(send_sem.at[phase], buffers[phase], buffers[phase].shape[0])

    barrier = pltpu.get_barrier_semaphore()
    for _, peer in con_peers + red_peers:
        pl.semaphore_signal(barrier, inc=1, device_id=peer, device_id_type=MESH)

    msg[...] = jnp.zeros_like(msg)
    rhs[...] = jnp.zeros_like(rhs)
    for load in loads:
        load.wait()
    for q in range(groups):
        msg[:, q * width : (q + 1) * width] = points[8 * q : 8 * q + 8, :]
    for p in range(n_part):
        rhs[p * per : p * per + 1, 0:width] = targets[...]
        rhs[p * per + 1 : (p + 1) * per, 0:width] = probes[p * (per - 1) : (p + 1) * (per - 1), :]
    msg[:, base : base + width] = rhs[0:8, 0:width]
    msg[0 : count - 8, base + width : base + 2 * width] = rhs[8:count, 0:width]

    row_at = lax.broadcasted_iota(jnp.int32, (count, 1), 0)
    lane_at = lax.broadcasted_iota(jnp.int32, (count, LANES), 1)
    mine = [(row_at >= p * per) & (row_at < (p + 1) * per) for p in range(n_part)]
    noise = jnp.zeros((count, 1), F32)
    for p in range(n_part):
        noise = jnp.where(mine[p], noise_var[p], noise)
    scales = []
    for p in range(n_part):
        length = jnp.full((1, TILE), lengthscale[p], F32)
        scales.append(((-0.5 * LOG2E) / (length * length), jnp.full((1, TILE), outputscale[p], F32)))
    product[...] = jnp.zeros_like(product)
    half = span // 2
    con_dt[NZ] = jnp.zeros_like(con_dt[NZ])
    for p in range(n_part):
        last = p * half + half - pair
        kept_odd[last : last + pair, :] = jnp.zeros((pair, wide), BF16)

    pl.semaphore_wait(barrier, n_red - 1 + n_con - 1)

    def send(phase, peer, src, dst, sem=None):
        pltpu.make_async_remote_copy(
            src_ref=src,
            dst_ref=dst,
            send_sem=send_sem.at[phase],
            recv_sem=recv_sem.at[phase] if sem is None else sem,
            device_id=peer,
            device_id_type=MESH,
        ).start()

    def to_con(phase, src, slots):
        for _, peer in con_peers:
            send(phase, peer, src, slots.at[me_con])

    def to_red(phase, src, slots):
        for _, peer in red_peers:
            send(phase, peer, src, slots.at[me_red])

    to_red(1, msg.at[:, 0:base], red_in)
    for _, peer in con_peers:
        send(0, peer, msg, con_in.at[me_con], con_sem.at[me_con])
    to_red(9, msg.at[:, base:], red_rhs_in)
    con_in[me_con] = msg[...]
    red_in[me_red] = msg[:, 0:base]
    red_rhs_in[me_red] = msg[:, base:]

    pad = jnp.zeros((TILE - 6 * feats - 16, LANES), F32)

    def con_wait(slot):
        pltpu.make_async_copy(con_in.at[slot], con_in.at[slot], con_sem.at[slot]).wait()

    def prepare(t, z, lhs):
        for c in range(CORES):
            slot = z * CORES + c
            x = jnp.concatenate(
                [con_in[slot, :, q * width : q * width + LANES] for q in range(groups)], axis=0
            )
            hi, mid, low = split3(x)
            norms = norm_rows(split3(jnp.sum(x * x, axis=0, keepdims=True)), False)
            full = jnp.concatenate([hi, hi, mid, hi, mid, low, norms, pad], axis=0)
            lhs[c * width : (c + 1) * width, :] = jnp.transpose(full)[0:width].astype(BF16)
            con_dt[t, 0:8, c * width : (c + 1) * width] = con_in[slot, :, base : base + width]
            con_dt[t, 8:count, c * width : (c + 1) * width] = con_in[
                slot, 0 : count - 8, base + width : base + 2 * width
            ]

    tiles = [slice(jb * TILE, (jb + 1) * TILE) for jb in range(wide // TILE)]

    def distances(lhs, dist):
        for jb, cols in enumerate(tiles):
            dist[jb] = jnp.dot(lhs[...], red_op[:, cols], preferred_element_type=F32)

    def exponentials(i, dist, kept):
        for jb, cols in enumerate(tiles):
            for r in range(pair // CHUNK):
                part = dist[jb, r * CHUNK : (r + 1) * CHUNK, :]
                for p in range(n_part):
                    kern = (scales[p][1] * jnp.exp2(part * scales[p][0])).astype(BF16)
                    at = pl.multiple_of(i * pair, CHUNK) + p * half + r * CHUNK
                    kept[pl.ds(at, CHUNK), cols] = kern

    def multiply(t, i, kept):
        low = con_dt[t, :, 0:pair]
        sides = [jnp.where(mine[p], low, 0.0).astype(BF16) for p in range(n_part)]
        for cols in tiles:
            total = product[:, cols]
            for p in range(n_part):
                at = pl.multiple_of(i * pair, CHUNK) + p * half
                total = total + jnp.dot(sides[p], kept[pl.ds(at, pair), cols], preferred_element_type=F32)
            product[:, cols] = total

    con_wait(at_z * CORES + 1 - core)
    prepare(0, at_z, lhs_even)

    arrive(recv_sem.at[1], red_in, n_red)
    for k in range(n_red):
        for q in range(groups):
            red_x[8 * q : 8 * q + 8, k * width : (k + 1) * width] = red_in[k, :, q * width : (q + 1) * width]
    x = red_x[...]
    hi, mid, low = split3(x)
    norms = norm_rows(split3(jnp.sum(x * x, axis=0, keepdims=True)), True)
    hi, mid, low = (-2.0 * hi, -2.0 * mid, -2.0 * low)
    pad2 = jnp.zeros((TILE - 6 * feats - 16, wide), F32)
    red_op[...] = jnp.concatenate([hi, mid, hi, low, mid, hi, norms, pad2], axis=0).astype(BF16)

    distances(lhs_even, dist_even)

    last = NZ // 2 - 1

    def steps(i, _):
        z = near_z(2 * i + 1)
        con_wait(z * CORES)
        con_wait(z * CORES + 1)
        multiply(lax.rem(2 * i + NZ, NZ + 1), lax.rem(i + last, NZ // 2), kept_odd)
        prepare(2 * i + 1, z, lhs_odd)
        distances(lhs_odd, dist_odd)
        exponentials(i, dist_even, kept_even)
        z = near_z(2 * i + 2)

        @pl.when(i < last)
        def _():
            con_wait(z * CORES)
            con_wait(z * CORES + 1)

        multiply(2 * i, i, kept_even)
        prepare(2 * i + 2, z, lhs_even)
        distances(lhs_even, dist_even)
        exponentials(i, dist_odd, kept_odd)
        return 0

    lax.fori_loop(0, NZ // 2, steps, 0)
    multiply(NZ - 1, last, kept_odd)

    arrive(recv_sem.at[9], red_rhs_in, n_red)
    for k in range(n_red):
        red_d[0:8, k * width : (k + 1) * width] = red_rhs_in[k, :, 0:width]
        red_d[8:count, k * width : (k + 1) * width] = red_rhs_in[k, 0 : count - 8, width : 2 * width]

    def chunk_out(k, buf):
        buf[k, :, 0:width] = product[:, k * width : (k + 1) * width]
        buf[k, :, width:LANES] = jnp.zeros((count, LANES - width), F32)

    def to_row(column, offset):
        return jnp.sum(jnp.where(lane_at == row_at + offset, column, 0.0), axis=0, keepdims=True)

    def to_column(row, offset):
        return jnp.sum(jnp.where(lane_at == row_at + offset, row, 0.0), axis=1, keepdims=True)

    own_d = rhs[...]
    d_red = red_d[...]
    for k in range(n_red):
        chunk_out(k, rs_send)
    for at, peer in red_peers:
        send(2, peer, rs_send.at[at], rs_recv.at[me_red])
    rs_recv[me_red] = rs_send[me_red]
    for t in range(NZ):
        con_d[:, t * pair : (t + 1) * pair] = con_dt[t, :, 0:pair]
    d_con = con_d[...]
    arrive(recv_sem.at[2], rs_recv, n_red)
    a_own = jnp.sum(rs_recv[...], axis=0) + noise * own_d
    ag_send[...] = a_own

    def over_lanes(v):
        return jnp.sum(jnp.where(lane_at < width, v, 0.0), axis=1, keepdims=True)

    dd, da, aa = over_lanes(own_d * own_d), over_lanes(own_d * a_own), over_lanes(a_own * a_own)
    guess = jnp.where(da * 16.0 > dd, dd / jnp.where(da > 0.0, da, 1.0), 0.0)
    left = own_d - guess * a_own
    mom_send[...] = (
        to_row(guess, 0)
        + to_row(over_lanes(left * left), count)
        + to_row(over_lanes(left * a_own), 2 * count)
        + to_row(aa, 3 * count)
        + to_row(dd, 4 * count)
        + to_row(da, 5 * count)
    )
    to_red(5, mom_send, mom_recv)
    to_con(3, ag_send, ag_con)
    to_red(4, ag_send, ag_red)
    mom_recv[me_red] = mom_send[...]
    ag_con[me_con] = ag_send[...]
    ag_red[me_red] = ag_send[...]

    def merge(slots):
        rows = jnp.concatenate([slots[k] for k in range(slots.shape[0])], axis=0)

        def field(f):
            return rows if f == 0 else pltpu.roll(rows, LANES - f * count, 1)

        def add(v):
            return jnp.sum(v, axis=0, keepdims=True)

        dd, da = add(field(4)), add(field(5))
        ok = da * 16.0 > dd
        guess = jnp.where(ok, dd / jnp.where(ok, da, 1.0), 0.0)
        off = field(0) - guess
        a_sq, cross, base_sq = field(3), field(2), field(1)
        cross_new = cross + off * a_sq
        base_new = base_sq + off * (cross + cross_new)
        return guess, add(base_new), add(cross_new), add(a_sq), dd, da

    arrive(recv_sem.at[5], mom_recv, n_red)
    packed = jnp.zeros((1, LANES), F32)
    lane_row = lax.broadcasted_iota(jnp.int32, (1, LANES), 1)
    for f, value in enumerate(merge(mom_recv)):
        moved = value if f == 0 else pltpu.roll(value, f * count, 1)
        packed = jnp.where((lane_row >= f * count) & (lane_row < (f + 1) * count), moved, packed)
    sum_send[...] = packed
    to_con(10, sum_send, sum_recv)
    sum_recv[me_con] = sum_send[...]

    arrive(recv_sem.at[3], ag_con, n_con)
    for t in range(NZ):
        for c in range(CORES):
            at = t * pair + c * width
            con_a[:, at : at + width] = ag_con[near[t] * CORES + c, :, 0:width]
    arrive(recv_sem.at[4], ag_red, n_red)
    for k in range(n_red):
        red_a[:, k * width : (k + 1) * width] = ag_red[k, :, 0:width]
    arrive(recv_sem.at[10], sum_recv, n_con)
    step_row, fresh_row, _, _, norm_row, _ = merge(sum_recv)
    step_size = to_column(step_row, 0)
    fresh_norm, res_norm = to_column(fresh_row, 0), to_column(norm_row, 0)
    r_con = d_con - step_size * con_a[...]
    r_red = d_red - step_size * red_a[...]
    r_own = own_d - step_size * a_own
    beta = fresh_norm / res_norm
    d1_con = r_con + beta * d_con
    for p in range(n_part):
        low = jnp.where(mine[p], d1_con, 0.0).astype(BF16)
        for t in range(NZ):
            at = (t % 2) * n_part * half + p * half + (t // 2) * pair
            blocks[:, at : at + pair] = low[:, t * pair : (t + 1) * pair]
    d1_red = r_red + beta * d_red
    d1_own = r_own + beta * own_d

    done = 0
    for jb in range(wide // TILE):
        cols = slice(jb * TILE, (jb + 1) * TILE)
        product[:, cols] = jnp.dot(
            blocks[:, 0 : n_part * half], kept_even[:, cols], preferred_element_type=F32
        ) + jnp.dot(blocks[:, n_part * half :], kept_odd[:, cols], preferred_element_type=F32)
        while (done + 1) * width <= (jb + 1) * TILE:
            chunk_out(done, rs2_send)
            done += 1
    crv_send[...] = to_row(jnp.sum(d1_red * product[...], axis=1, keepdims=True), 0)
    to_red(8, crv_send, crv_recv)
    for at, peer in red_peers:
        send(6, peer, rs2_send.at[at], rs2_recv.at[me_red])
    crv_recv[me_red] = crv_send[...]
    norm1 = to_row(jnp.sum(d1_red * d1_red, axis=1, keepdims=True), count)
    arrive(recv_sem.at[8], crv_recv, n_red)
    fin_send[...] = jnp.sum(crv_recv[...], axis=0) + norm1
    to_con(7, fin_send, fin_recv)
    fin_recv[me_con] = fin_send[...]
    rs2_recv[me_red] = rs2_send[me_red]
    arrive(recv_sem.at[6], rs2_recv, n_red)
    a1_own = jnp.sum(rs2_recv[...], axis=0) + noise * d1_own
    drain((0, 1, 2, 3, 4, 5, 6, 8, 9, 10))
    arrive(recv_sem.at[7], fin_recv, n_con)
    total = jnp.sum(fin_recv[...], axis=0)
    step1 = fresh_norm / (to_column(total, 0) + noise * to_column(total, count))
    sol = step_size * own_d + step1 * d1_own
    res = r_own - step1 * a1_own
    sol_out[...] = sol[:, 0:width]
    res_out[...] = res[:, 0:width]
    drain((7,))


def solution(mesh):
    n_red, n_con = NX * NY, NZ * CORES

    def on_device(points, targets, probes, lengthscale, outputscale, noise_var):
        feats, width = points.shape
        n_part = lengthscale.shape[0]
        per = probes.shape[0] // n_part + 1
        count = n_part * per
        pair, span, wide = CORES * width, n_con * width, n_red * width
        whole = pl.cdiv(feats * width // 8 + 2 * width, LANES) * LANES
        base = feats * width // 8
        vmem = pl.BlockSpec(memory_space=pltpu.VMEM)
        anywhere = pl.BlockSpec(memory_space=pl.ANY)
        out = jax.ShapeDtypeStruct((count, width), F32)

        def slots(n, *shape):
            return pltpu.VMEM((n, *(shape or (count, LANES))), F32)

        row = pltpu.VMEM((1, LANES), F32)
        return pl.pallas_call(
            functools.partial(kernel, width, per),
            out_shape=(out, out),
            in_specs=[anywhere] * 6,
            out_specs=(vmem, vmem),
            scratch_shapes=[
                pltpu.VMEM((feats, width), F32),
                pltpu.VMEM((1, width), F32),
                pltpu.VMEM(probes.shape, F32),
                pltpu.SMEM((n_part,), F32),
                pltpu.SMEM((n_part,), F32),
                pltpu.SMEM((n_part,), F32),
                pltpu.VMEM((count, LANES), F32),
                pltpu.VMEM((8, whole), F32),
                slots(n_con, 8, whole),
                slots(n_red, 8, base),
                slots(n_red, 8, whole - base),
                pltpu.VMEM((pair, TILE), BF16),
                pltpu.VMEM((pair, TILE), BF16),
                pltpu.VMEM((NZ + 1, count, TILE), F32),
                pltpu.VMEM((feats, wide), F32),
                pltpu.VMEM((TILE, wide), BF16),
                pltpu.VMEM((count, span), F32),
                pltpu.VMEM((count, wide), F32),
                pltpu.VMEM((count, span), F32),
                pltpu.VMEM((count, wide), F32),
                pltpu.VMEM((count, n_part * span), BF16),
                pltpu.VMEM((wide // TILE, pair, TILE), F32),
                pltpu.VMEM((wide // TILE, pair, TILE), F32),
                pltpu.VMEM((n_part * span // 2, wide), BF16),
                pltpu.VMEM((n_part * span // 2, wide), BF16),
                pltpu.VMEM((count, wide), F32),
                slots(n_red),
                slots(n_red),
                pltpu.VMEM((count, LANES), F32),
                slots(n_con),
                slots(n_red),
                row,
                slots(n_red, 1, LANES),
                row,
                slots(n_con, 1, LANES),
                slots(n_red),
                slots(n_red),
                row,
                slots(n_red, 1, LANES),
                row,
                slots(n_con, 1, LANES),
                pltpu.SemaphoreType.DMA((6,)),
                pltpu.SemaphoreType.DMA((11,)),
                pltpu.SemaphoreType.DMA((11,)),
                pltpu.SemaphoreType.DMA((n_con,)),
            ],
            compiler_params=pltpu.CompilerParams(
                collective_id=0, has_side_effects=True, vmem_limit_bytes=56 * 2**20
            ),
            name="cg_solve",
        )(points, targets[None, :], probes, lengthscale, outputscale, noise_var)

    both = P(None, ("row", "col"))
    return jax.shard_map(
        on_device,
        mesh=mesh,
        in_specs=(both, P(("row", "col")), both, P(), P(), P()),
        out_specs=(both, both),
        check_vma=False,
    )
```
